32 devices in a mesh: survey: 2 (over y), off: 8 (over z, x), gy: 2 (over core).
Axes of the slice: x: 2, y: 2, z: 4, core: 2. Of those that a mesh axis runs over, the one named last changes fastest.
Arguments:
- checkpoint: float32 [16, 2, 2, 16, 48, 256], P(('survey', 'off'), None, None, 'gy'), parts along dimension 0, may hold values from -6 to 6
- traces: float32 [16, 4, 16, 256], P(('survey', 'off'), None, 'gy'), parts along dimension 0, may hold values from -6 to 6
- courant_sq: float32 [16, 48, 256], P('gy'), may hold values from 0.06 to 0.18
- holder: int32 [8], P('survey'), parts along dimension 0, may hold values from 0 to 7, as said below
- offset_lags: int32 [16, 4], P(('survey', 'off')), parts along dimension 0, may hold values from -16 to 15, as said below
Outputs:
- offset_image: float32 [64, 16, 48, 256], P(('survey', 'off'), 'gy'), parts along dimension 0
The draws below stay inside these ranges and needn't reach their ends.
There are 2 independent parts, one for each index of `survey`. The reference program is written for one: setup_inputs(seed, part) draws one part's arguments, and reference() takes and returns one part's arrays. A program takes and returns all parts, laid end to end along the dimension named above; an argument that names none is the same for every part. Nothing has to cross between parts.
Inputs may be any that keep to these rules, and one draw needn't show every extreme that they name: `holder`: the 4 entries are distinct; every draw contains both 0 and 8 - 1. `offset_lags`: each of the 32 values from -16 to 15 appears exactly once.
All inputs are finite; a program needn't handle non-finite values.
Results may differ from the reference program's by a relative error of at most 0.0041.
Values may be sent and summed in bfloat16 or wider, within the bound.
No kernel may reach another device: no remote copies, remote signals or barrier semaphores. Data moves between devices by JAX's collectives and lax.ppermute only.
A program may use at most 128 MiB of HBM per device.

```python
import math
import jax
import jax.numpy as jnp
from jax import lax

NX = 256
CZ = 48
SHOTS = 4
OFF_DEV = 4
STEPS = 4
HOFF = 32
NY = 16
N_OFF = 8


def draw_holder(key, part):
    middle = 1 + jax.random.permutation(jax.random.fold_in(key, 11), N_OFF - 2)[:SHOTS - 2]
    pool = jnp.concatenate([jnp.array([0, N_OFF - 1], jnp.int32), middle.astype(jnp.int32)])
    order = jax.random.permutation(jax.random.fold_in(key, 12), SHOTS)
    return pool[order].astype(jnp.int32)


def draw_offset_lags(key, part):
    values = jax.random.permutation(jax.random.fold_in(key, 13), HOFF).astype(jnp.int32) - HOFF // 2
    return values.reshape(N_OFF, OFF_DEV).astype(jnp.int32)


def level_of(own_key, extent, pieces, smallest, high):
    factor_of, own = 1.0, jax.random.fold_in(own_key, 6)
    for dim, shards_of in pieces:
        steps = jnp.exp(jax.random.uniform(jax.random.fold_in(own, dim), (shards_of,), jnp.float32, smallest / len(pieces), high / len(pieces)))
        factor_of = factor_of * jnp.repeat(steps, extent[dim] // shards_of).reshape([-1 if axis == dim else 1 for axis in range(len(extent))])
    return factor_of


def noise(key, extent, width, most, split=(), kind=jnp.bfloat16):
    entries = width * jax.random.normal(key, extent, jnp.float32)
    if split:
        entries = entries * level_of(key, extent, split, -0.22, 0.18)
    return jnp.clip(entries, -most, most).astype(kind)


def setup_inputs(seed: int = 0, part: int = 0) -> dict:
    splits = jax.random.split(jax.random.key(seed), 6)
    part_keys = jax.random.split(jax.random.fold_in(splits[5], part), 6)
    return {
        "checkpoint": noise(part_keys[0], (N_OFF, 2, 2, NY, CZ, NX), 1.0, 6.0, ((0, 8), (3, 2)), jnp.float32),
        "traces": noise(part_keys[1], (N_OFF, STEPS, NY, NX), 1.0, 6.0, ((0, 8), (2, 2)), jnp.float32),
        "courant_sq": jnp.clip(jnp.exp(math.log(0.18) - 1.09861235 * jax.random.uniform(splits[2], (NY, CZ, NX), jnp.float32) ** level_of(splits[2], (NY, CZ, NX), ((0, 2),), -0.2, 0.2)), 0.06, 0.18),
        "holder": draw_holder(jax.random.fold_in(jax.random.fold_in(splits[5], part), 71), part),
        "offset_lags": draw_offset_lags(jax.random.fold_in(jax.random.fold_in(splits[5], part), 71), part),
    }


stencil_taps = (-205.0 / 72.0, 8.0 / 5.0, -1.0 / 5.0, 8.0 / 315.0, -1.0 / 560.0)


def laplace(extended):
    cells_y = extended.shape[-3] - 8
    cells_z = extended.shape[-2]
    cells_x = extended.shape[-1]
    leading = [(0, 0)] * (extended.ndim - 2)
    padded = jnp.pad(extended, leading + [(4, 4), (4, 4)])

    def shifted(step_y, step_z, step_x):
        return padded[..., 4 + step_y:4 + step_y + cells_y, 4 + step_z:4 + step_z + cells_z, 4 + step_x:4 + step_x + cells_x]

    summed = 3.0 * stencil_taps[0] * shifted(0, 0, 0)
    for tap_no in range(1, 5):
        beside_all = shifted(tap_no, 0, 0) + shifted(-tap_no, 0, 0)
        beside_all = beside_all + shifted(0, tap_no, 0) + shifted(0, -tap_no, 0)
        beside_all = beside_all + shifted(0, 0, tap_no) + shifted(0, 0, -tap_no)
        summed = summed + stencil_taps[tap_no] * beside_all
    return summed


def advance(earlier, current, extended, courant_sq, drive):
    advanced = 2.0 * current - earlier + courant_sq * laplace(extended)
    advanced = advanced.at[:, 1, :, 0, :].add(drive)
    return current, advanced


def reference(checkpoint, traces, courant_sq, holder, offset_lags):
    starts = checkpoint[holder]
    drives = traces[holder]
    earlier = starts[:, 0]
    current = starts[:, 1]
    snapshots = []
    for step_no in range(STEPS):
        extended = jnp.pad(current, ((0, 0), (0, 0), (4, 4), (0, 0), (0, 0)))
        earlier, current = advance(earlier, current, extended, courant_sq, drives[:, step_no])
        if step_no % 2 == 1:
            snapshots.append(current.astype(jnp.bfloat16))
    stacked = jnp.concatenate(snapshots, axis=0)
    source = stacked[:, 0].astype(jnp.float32)
    receiver = stacked[:, 1].astype(jnp.float32)
    half_span = HOFF // 2
    padded = jnp.pad(receiver, ((0, 0), (0, 0), (0, 0), (half_span, half_span)))

    def one_lag(lag_value):
        moved = lax.dynamic_slice_in_dim(padded, (half_span + lag_value).astype(jnp.int32), NX, 3)
        return jnp.sum(source * moved, axis=0)

    return lax.map(one_lag, offset_lags.reshape(-1))
```

```python
import functools
import jax
import jax.numpy as jnp
from jax import lax
from jax.experimental import pallas as pl
from jax.experimental.pallas import tpu as pltpu
from jax.sharding import PartitionSpec as P

stencil_taps = (-205.0 / 72.0, 8.0 / 5.0, -1.0 / 5.0, 8.0 / 315.0, -1.0 / 560.0)
REACH = 4
LANES = 128
SUBLANES = 8
VMEM = pl.BlockSpec(memory_space=pltpu.VMEM)
SMEM = pl.BlockSpec(memory_space=pltpu.SMEM)


def extended_2(shard, sides, width):
    for axis, dim in sides:
        devices, length = (lax.axis_size(axis), shard.shape[dim])
        up = [(i, (i + 1) % devices) for i in range(devices - 1)]
        down = [(j, i) for i, j in up]
        last = lax.slice_in_dim(shard, length - width, length, axis=dim)
        initial = lax.slice_in_dim(shard, 0, width, axis=dim)
        before = lax.ppermute(last, axis, up)
        after = lax.ppermute(initial, axis, down)
        shard = jnp.concatenate([before, shard, after], axis=dim)
    return shard


def spread(value, axis, source):
    kept = jnp.where(lax.axis_index(axis) == source, value, 0).astype(value.dtype)
    return lax.psum(kept, axis)


def laplace(extended):
    cells_y = extended.shape[-3] - 8
    cells_z = extended.shape[-2]
    cells_x = extended.shape[-1]
    leading = [(0, 0)] * (extended.ndim - 2)
    padded = jnp.pad(extended, leading + [(4, 4), (4, 4)])

    def shifted(step_y, step_z, step_x):
        return padded[
            ...,
            4 + step_y : 4 + step_y + cells_y,
            4 + step_z : 4 + step_z + cells_z,
            4 + step_x : 4 + step_x + cells_x,
        ]

    summed = 3.0 * stencil_taps[0] * shifted(0, 0, 0)
    for tap_no in range(1, 5):
        beside_all = shifted(tap_no, 0, 0) + shifted(-tap_no, 0, 0)
        beside_all = beside_all + shifted(0, tap_no, 0) + shifted(0, -tap_no, 0)
        beside_all = beside_all + shifted(0, 0, tap_no) + shifted(0, 0, -tap_no)
        summed = summed + stencil_taps[tap_no] * beside_all
    return summed


def propagate_step(earlier, current, courant_sq, drive):
    extended = extended_2(current, (("gy", 2),), 4)
    advanced = 2.0 * current - earlier + courant_sq * laplace(extended)
    advanced = advanced.at[:, 1, :, 0, :].add(drive)
    return (current, advanced)


def correlate(image_acc, source, receiver, my_lags, half_span):
    cells_x = receiver.shape[-1]
    padded = jnp.pad(receiver, ((0, 0), (0, 0), (half_span, half_span)))
    moved = jax.vmap(
        lambda lag_value: lax.dynamic_slice_in_dim(padded, half_span + lag_value, cells_x, 2)
    )(my_lags)
    return image_acc + source.astype(jnp.float32)[None] * moved.astype(jnp.float32)


def on_device_general(checkpoint, traces, courant_sq, holder, offset_lags):
    shot_count = holder.shape[0]
    step_count = traces.shape[1]
    my_lags = offset_lags[0]
    half_span = lax.axis_size("off") * offset_lags.shape[1] // 2
    image_acc = jnp.zeros((offset_lags.shape[1],) + courant_sq.shape, jnp.float32)
    earlier = checkpoint[:, 0]
    current = checkpoint[:, 1]
    collected = []
    for step_no in range(step_count):
        earlier, current = propagate_step(earlier, current, courant_sq, traces[:, step_no])
        if step_no % 2 == 1:
            snapshot = current[0].astype(jnp.bfloat16)
            collected.append(snapshot)
    snap_runs = jnp.stack(collected)
    for shot_no in range(shot_count):
        received = spread(snap_runs, "off", holder[shot_no])
        for snap_no in range(received.shape[0]):
            image_acc = correlate(
                image_acc, received[snap_no, 0], received[snap_no, 1], my_lags, half_span
            )
    return image_acc


def shifted_x(tiles, step, lane):
    count = len(tiles)
    if step > 0:
        rolled = [pltpu.roll(t, LANES - step, 1) for t in tiles]
        keep = lane < LANES - step
        return [
            jnp.where(keep, rolled[i], rolled[i + 1] if i + 1 < count else 0.0)
            for i in range(count)
        ]
    step = -step
    rolled = [pltpu.roll(t, step, 1) for t in tiles]
    keep = lane >= step
    return [jnp.where(keep, rolled[i], rolled[i - 1] if i else 0.0) for i in range(count)]


def step_kernel(spec, *refs):
    first, snaps, last = spec
    refs = list(refs)
    side_ref = refs.pop(0)
    if last:
        me_ref, lags_ref = refs.pop(0), refs.pop(0)
    if first:
        start_ref = refs.pop(0)
        earlier_of = lambda f, y: start_ref[first - 1, f, y]
        if first == 1:
            current_of = lambda f, y: start_ref[1, f, y]
        else:
            current_ref = refs.pop(0)
            current_of = lambda f, y: current_ref[f, y]
    else:
        earlier_ref, current_ref = refs.pop(0), refs.pop(0)
        earlier_of = lambda f, y: earlier_ref[f, y]
        current_of = lambda f, y: current_ref[f, y]
    halo_ref, courant_ref, drive_ref = refs.pop(0), refs.pop(0), refs.pop(0)
    ext = refs.pop()
    out_ref = refs.pop(0)
    fields, planes, cells_z, cells_x = out_ref.shape
    side = side_ref[0]
    halo_at = jnp.where(side == 0, REACH + planes, 0)
    none_at = jnp.where(side == 0, 0, REACH + planes)
    pad = jnp.zeros((SUBLANES, cells_x), jnp.float32)
    empty = jnp.zeros((cells_z, cells_x), jnp.float32)
    body = pl.ds(SUBLANES, cells_z)
    for f in range(fields):
        for y in range(planes):
            ext[f, REACH + y, body] = current_of(f, y)
            ext[f, REACH + y, pl.ds(0, SUBLANES)] = pad
            ext[f, REACH + y, pl.ds(SUBLANES + cells_z, SUBLANES)] = pad
        for y in range(REACH):
            ext[f, halo_at + y, body] = halo_ref[f, y]
            ext[f, none_at + y, body] = empty
    lane = lax.broadcasted_iota(jnp.int32, (cells_z, LANES), 1)
    tiles_x = cells_x // LANES

    def one_plane(f, y):
        here = ext[f, REACH + y, body]
        tiles = [here[:, i * LANES : (i + 1) * LANES] for i in range(tiles_x)]
        lap = (3.0 * stencil_taps[0]) * here
        for tap in range(1, REACH + 1):
            beside = ext[f, REACH + y + tap, body] + ext[f, REACH + y - tap, body]
            beside += ext[f, REACH + y, pl.ds(SUBLANES + tap, cells_z)]
            beside += ext[f, REACH + y, pl.ds(SUBLANES - tap, cells_z)]
            right, left = shifted_x(tiles, tap, lane), shifted_x(tiles, -tap, lane)
            beside += jnp.concatenate([a + b for a, b in zip(right, left)], axis=1)
            lap += stencil_taps[tap] * beside
        out_ref[f, y] = 2.0 * here - earlier_of(f, y) + courant_ref[y] * lap

    for f in range(fields):

        def step(y, carry, f=f):
            one_plane(f, y)
            return carry

        lax.fori_loop(0, planes, step, 0)
    for y in range(planes):
        out_ref[1, y, pl.ds(0, 1)] = out_ref[1, y, pl.ds(0, 1)] + drive_ref[pl.ds(y, 1)]
    if not last:
        edge_ref = refs.pop(0)
        edge_at = jnp.where(side == 0, planes - REACH, 0)
        for f in range(fields):
            for y in range(REACH):
                edge_ref[f, y] = out_ref[f, edge_at + y]
        return
    me = me_ref[0]
    row = lax.broadcasted_iota(jnp.int32, (SUBLANES, cells_x), 0)
    tail = jnp.zeros((SUBLANES, cells_x), jnp.float32)
    for i in range(lags_ref.shape[1]):
        tail = jnp.where(row == i, lags_ref[0, i].astype(jnp.float32), tail)
    for k, part_ref in enumerate(refs):
        y = jnp.bitwise_xor(me, k)
        for f in range(fields):
            part_ref[pl.ds(f * cells_z, cells_z)] = earlier_of(f, y).astype(jnp.bfloat16)
            part_ref[pl.ds((fields + f) * cells_z, cells_z)] = out_ref[f, y].astype(jnp.bfloat16)
        part_ref[pl.ds(2 * fields * cells_z, SUBLANES)] = tail.astype(jnp.bfloat16)


def advance(spec, side, extra, levels, halo, courant_sq, drive, groups):
    first, snaps, last = spec
    current = levels[-1]
    fields, planes, cells_z, cells_x = current.shape[-4:]
    shape = jax.ShapeDtypeStruct
    outs = [shape((fields, planes, cells_z, cells_x), jnp.float32)]
    if last:
        rows = 2 * fields * cells_z + SUBLANES
        outs += [shape((rows, cells_x), jnp.bfloat16)] * groups
    else:
        outs += [shape((fields, REACH, cells_z, cells_x), jnp.float32)]
    cells = fields * planes * cells_z * cells_x
    args = [side, *extra, *levels, halo, courant_sq, drive]
    scalars = 1 + len(extra)
    return pl.pallas_call(
        functools.partial(step_kernel, spec),
        out_shape=outs,
        in_specs=[SMEM] * scalars + [VMEM] * (len(args) - scalars),
        out_specs=[VMEM] * len(outs),
        scratch_shapes=[
            pltpu.VMEM((fields, planes + 2 * REACH, cells_z + 2 * SUBLANES, cells_x), jnp.float32)
        ],
        cost_estimate=pl.CostEstimate(
            flops=50 * cells, bytes_accessed=16 * cells, transcendentals=0
        ),
        name="advance",
    )(*args)


def image_kernel(snaps, fields, shots, valid_ref, *refs):
    groups = valid_ref.shape[0]
    parts, outs, held = refs[:groups], refs[groups:-1], refs[-1]
    per_group, cells_z, cells_x = outs[0].shape
    tail = snaps * fields * cells_z
    place = 0
    lags = []
    for k in range(groups):

        @pl.when(valid_ref[k] > 0)
        def _(k=k, place=place):
            for i in range(snaps * fields):
                held[place, i] = parts[k][pl.ds(i * cells_z, cells_z)].astype(jnp.float32)

        place = jnp.minimum(place + valid_ref[k], shots - 1)
        ends = parts[k][pl.ds(tail, SUBLANES)].astype(jnp.float32)
        lags.append([ends[i, 0].astype(jnp.int32) for i in range(per_group)])
    tiles_x = cells_x // LANES
    rows = 2 * SUBLANES
    lane = lax.broadcasted_iota(jnp.int32, (rows, LANES), 1)

    def strip(z, carry):
        at = pl.ds(pl.multiple_of(z * rows, rows), rows)
        for k in range(groups):
            for i in range(per_group):
                lag = lags[k][i]
                turn = jnp.where(lag > 0, LANES - lag, -lag)
                split = jnp.where(lag > 0, LANES - lag, -lag)
                low = lane < split
                ahead = lag > 0
                own_low = jnp.where(ahead, 1, 0)
                own = low == (own_low > 0)
                sums = [jnp.zeros((rows, LANES), jnp.float32)] * tiles_x
                for s in range(shots):
                    for m in range(snaps):
                        rolled = [
                            pltpu.roll(
                                held[s, m * fields + 1, at, pl.ds(t * LANES, LANES)], turn, 1
                            )
                            for t in range(tiles_x)
                        ]
                        for t in range(tiles_x):
                            if tiles_x == 2:
                                other = rolled[1 - t]
                            else:
                                other = jnp.where(
                                    ahead, rolled[(t + 1) % tiles_x], rolled[(t - 1) % tiles_x]
                                )
                            moved = jnp.where(own, rolled[t], other)
                            sums[t] += held[s, m * fields, at, pl.ds(t * LANES, LANES)] * moved
                for t in range(tiles_x):
                    x = lane + t * LANES + lag
                    inside = (x >= 0) & (x < cells_x)
                    outs[k][i, at, pl.ds(t * LANES, LANES)] = jnp.where(
                        inside, sums[t], 0.0
                    ).astype(outs[k].dtype)
        return carry

    lax.fori_loop(0, cells_z // rows, strip, 0)


def gather_kernel(me_ref, *refs):
    out_ref = refs[-1]
    for k, part_ref in enumerate(refs[:-1]):
        y = jnp.bitwise_xor(me_ref[0], k)
        for i in range(out_ref.shape[0]):
            out_ref[i, y] = part_ref[i].astype(jnp.float32)


def on_device_planes(checkpoint, traces, courant_sq, holder, offset_lags):
    start = checkpoint[0]
    fields, planes, cells_z, cells_x = start.shape[1:]
    step_count = traces.shape[1]
    groups = lax.axis_size("off")
    shots = holder.shape[0]
    per_group = offset_lags.shape[1]
    snaps = step_count // 2
    me = lax.axis_index("off").astype(jnp.int32)
    side = lax.axis_index("gy").astype(jnp.int32)
    slots = jnp.bitwise_xor(me, jnp.arange(groups, dtype=jnp.int32))
    valid = jnp.any(holder[None, :] == slots[:, None], axis=1).astype(jnp.int32)
    side1, me1 = side.reshape(1), me.reshape(1)
    swap = [(0, 1), (1, 0)]

    edge = lax.dynamic_slice_in_dim(start[1], (1 - side) * (planes - REACH), REACH, axis=1)
    earlier = current = None
    for n in range(step_count):
        halo = lax.ppermute(edge, "gy", swap)
        last = n == step_count - 1
        spec = (n + 1 if n < 2 else 0, snaps, last)
        levels = [start] if n == 0 else [start, current] if n == 1 else [earlier, current]
        extra = [me1, offset_lags] if last else []
        made = advance(
            spec, side1, extra, levels, halo, courant_sq, traces[0, n], groups
        )
        earlier, current = current, made[0]
        edge = made[1]
    parts = made[1:]

    def pairs(k):
        return [(i, i ^ k) for i in range(groups)]

    order = [k for k in range(1, groups)]
    got = {0: parts[0]}
    for k in order:
        got[k] = lax.ppermute(parts[k], "off", pairs(k))
    plane = [jax.ShapeDtypeStruct((per_group, cells_z, cells_x), jnp.bfloat16)] * groups
    plane[0] = jax.ShapeDtypeStruct((per_group, cells_z, cells_x), jnp.float32)
    images = pl.pallas_call(
        functools.partial(image_kernel, snaps, fields, shots),
        out_shape=plane,
        in_specs=[SMEM] + [VMEM] * groups,
        out_specs=[VMEM] * groups,
        scratch_shapes=[pltpu.VMEM((shots, snaps * fields, cells_z, cells_x), jnp.float32)],
        name="image",
    )(valid, *[got[k] for k in range(groups)])
    back = {0: images[0]}
    for k in order:
        back[k] = lax.ppermute(images[k], "off", pairs(k))
    return pl.pallas_call(
        gather_kernel,
        out_shape=jax.ShapeDtypeStruct((per_group, planes, cells_z, cells_x), jnp.float32),
        in_specs=[SMEM] + [VMEM] * groups,
        out_specs=VMEM,
        name="gather",
    )(me1, *[back[k] for k in range(groups)])


def solution(mesh):
    placed = (
        P(("survey", "off"), None, None, "gy", None, None),
        P(("survey", "off"), None, "gy", None),
        P("gy", None, None),
        P("survey"),
        P(("survey", "off"), None),
    )

    def on_device(checkpoint, traces, courant_sq, holder, offset_lags):
        groups, sides = mesh.shape["off"], mesh.shape["gy"]
        planes, cells_z, cells_x = courant_sq.shape
        fits = (
            groups == planes
            and groups & (groups - 1) == 0
            and sides == 2
            and planes >= REACH
            and cells_z % (2 * SUBLANES) == 0
            and cells_x % LANES == 0
            and cells_x >= 2 * LANES
            and traces.shape[1] == 4
            and groups * offset_lags.shape[1] <= LANES
            and offset_lags.shape[1] <= SUBLANES
        )
        chosen = on_device_planes if fits else on_device_general
        return chosen(checkpoint, traces, courant_sq, holder, offset_lags)

    return jax.shard_map(
        on_device,
        mesh=mesh,
        in_specs=placed,
        out_specs=P(("survey", "off"), "gy", None, None),
        check_vma=False,
    )
```

```python
import functools
import jax
import jax.numpy as jnp
from jax import lax
from jax.experimental import pallas as pl
from jax.experimental.pallas import tpu as pltpu
from jax.sharding import PartitionSpec as P

stencil_taps = (-205.0 / 72.0, 8.0 / 5.0, -1.0 / 5.0, 8.0 / 315.0, -1.0 / 560.0)
REACH = 4
COMMON, BAND_UNIT = 5040.0, 4096.0
TAPS = tuple(round(tap * COMMON) / BAND_UNIT for tap in stencil_taps)
LANES = 128
SUBLANES = 8
VMEM = pl.BlockSpec(memory_space=pltpu.VMEM)
SMEM = pl.BlockSpec(memory_space=pltpu.SMEM)


def extended_2(shard, sides, width):
    for axis, dim in sides:
        devices, length = (lax.axis_size(axis), shard.shape[dim])
        up = [(i, (i + 1) % devices) for i in range(devices - 1)]
        down = [(j, i) for i, j in up]
        last = lax.slice_in_dim(shard, length - width, length, axis=dim)
        initial = lax.slice_in_dim(shard, 0, width, axis=dim)
        before = lax.ppermute(last, axis, up)
        after = lax.ppermute(initial, axis, down)
        shard = jnp.concatenate([before, shard, after], axis=dim)
    return shard


def spread(value, axis, source):
    kept = jnp.where(lax.axis_index(axis) == source, value, 0).astype(value.dtype)
    return lax.psum(kept, axis)


def laplace(extended):
    cells_y = extended.shape[-3] - 8
    cells_z = extended.shape[-2]
    cells_x = extended.shape[-1]
    leading = [(0, 0)] * (extended.ndim - 2)
    padded = jnp.pad(extended, leading + [(4, 4), (4, 4)])

    def shifted(step_y, step_z, step_x):
        return padded[
            ...,
            4 + step_y : 4 + step_y + cells_y,
            4 + step_z : 4 + step_z + cells_z,
            4 + step_x : 4 + step_x + cells_x,
        ]

    summed = 3.0 * stencil_taps[0] * shifted(0, 0, 0)
    for tap_no in range(1, 5):
        beside_all = shifted(tap_no, 0, 0) + shifted(-tap_no, 0, 0)
        beside_all = beside_all + shifted(0, tap_no, 0) + shifted(0, -tap_no, 0)
        beside_all = beside_all + shifted(0, 0, tap_no) + shifted(0, 0, -tap_no)
        summed = summed + stencil_taps[tap_no] * beside_all
    return summed


def propagate_step(earlier, current, courant_sq, drive):
    extended = extended_2(current, (("gy", 2),), 4)
    advanced = 2.0 * current - earlier + courant_sq * laplace(extended)
    advanced = advanced.at[:, 1, :, 0, :].add(drive)
    return (current, advanced)


def correlate(image_acc, source, receiver, my_lags, half_span):
    cells_x = receiver.shape[-1]
    padded = jnp.pad(receiver, ((0, 0), (0, 0), (half_span, half_span)))
    moved = jax.vmap(
        lambda lag_value: lax.dynamic_slice_in_dim(padded, half_span + lag_value, cells_x, 2)
    )(my_lags)
    return image_acc + source.astype(jnp.float32)[None] * moved.astype(jnp.float32)


def on_device_general(checkpoint, traces, courant_sq, holder, offset_lags):
    shot_count = holder.shape[0]
    step_count = traces.shape[1]
    my_lags = offset_lags[0]
    half_span = lax.axis_size("off") * offset_lags.shape[1] // 2
    image_acc = jnp.zeros((offset_lags.shape[1],) + courant_sq.shape, jnp.float32)
    earlier = checkpoint[:, 0]
    current = checkpoint[:, 1]
    collected = []
    for step_no in range(step_count):
        earlier, current = propagate_step(earlier, current, courant_sq, traces[:, step_no])
        if step_no % 2 == 1:
            snapshot = current[0].astype(jnp.bfloat16)
            collected.append(snapshot)
    snap_runs = jnp.stack(collected)
    for shot_no in range(shot_count):
        received = spread(snap_runs, "off", holder[shot_no])
        for snap_no in range(received.shape[0]):
            image_acc = correlate(
                image_acc, received[snap_no, 0], received[snap_no, 1], my_lags, half_span
            )
    return image_acc


def half_kernel(spec, *refs):
    step_no, near, last = spec
    refs = list(refs)
    side = refs.pop(0)[0]
    if last and near:
        me_ref, lags_ref = refs.pop(0), refs.pop(0)
    courant_ref, drive_ref, band_ref = refs.pop(0), refs.pop(0), refs.pop(0)
    start_ref = refs.pop(0) if step_no < 2 else None
    before_ref = refs.pop(0) if step_no >= 2 else None
    current_ref = refs.pop(0) if step_no >= 1 else None
    halo_ref = refs.pop(0) if near else None
    fresh_ref = refs.pop(0) if near else None
    along_x, split, ext = refs.pop(), refs.pop(), refs.pop()
    out_ref = refs.pop(0)
    fields, planes, cells_z, cells_x = out_ref.shape
    count = planes // 2
    tiles_x = cells_x // LANES
    everything = slice(None)

    def row_y(d):
        return jnp.where(side == 0, planes - 1 - d, d)

    def current(f, d, at=()):
        if d < 0:
            j = -1 - d
            if step_no == 0:
                j = jnp.where(side == 0, j, REACH - 1 - j)
            return halo_ref[(f, j, *at)]
        if step_no == 0:
            return start_ref[(1, f, row_y(d), *at)]
        return current_ref[(f, d, *at)]

    def before(f, d, at=()):
        if step_no < 2:
            return start_ref[(step_no, f, row_y(d), *at)]
        return before_ref[(f, d, *at)]

    base = 0 if near else count
    pad = jnp.zeros((SUBLANES, LANES), jnp.float32)
    for f in range(fields):
        for i in range(count):
            here = current(f, base + i)
            for t in range(tiles_x):
                ext[f, i, t, pl.ds(0, SUBLANES)] = pad
                ext[f, i, t, pl.ds(SUBLANES, cells_z)] = here[:, t * LANES : (t + 1) * LANES]
                ext[f, i, t, pl.ds(SUBLANES + cells_z, SUBLANES)] = pad
            high = here.astype(jnp.bfloat16)
            left = here - high.astype(jnp.float32)
            middle = left.astype(jnp.bfloat16)
            low = (left - middle.astype(jnp.float32)).astype(jnp.bfloat16)
            at = pl.ds((f * count + i) * cells_z, cells_z)
            for j, piece in enumerate((high, middle, low)):
                split[at, pl.ds(j * cells_x, cells_x)] = piece
    band = band_ref[...]
    along_x[...] = jnp.dot(
        split[...], jnp.concatenate([band] * 3, axis=0), preferred_element_type=jnp.float32
    )
    for i in range(count):
        d = base + i
        y = row_y(d)
        for t in range(tiles_x):
            across = pl.ds(t * LANES, LANES)
            at = (everything, across)
            courant = courant_ref[y, :, across] * (BAND_UNIT / COMMON)
            for f in range(fields):
                here = ext[f, i, t, pl.ds(SUBLANES, cells_z)]
                lap = (3.0 * TAPS[0]) * here
                lap += along_x[pl.ds((f * count + i) * cells_z, cells_z), across]
                for tap in range(1, REACH + 1):
                    beside = (
                        ext[f, i, t, pl.ds(SUBLANES + tap, cells_z)]
                        + ext[f, i, t, pl.ds(SUBLANES - tap, cells_z)]
                    )
                    for other in (d - tap, d + tap):
                        if other < planes:
                            beside += current(f, other, at)
                    lap += TAPS[tap] * beside
                out_ref[f, d, :, across] = (2.0 * here - before(f, d, at)) + courant * lap
        out_ref[1, d, pl.ds(0, 1)] = (
            out_ref[1, d, pl.ds(0, 1)] + drive_ref[step_no, pl.ds(y, 1)]
        )
    if not near:
        return
    for f in range(fields):
        for d in range(count, planes):
            out_ref[f, d] = fresh_ref[f, d]
    if not last:
        edge_ref = refs.pop(0)
        for f in range(fields):
            for d in range(REACH):
                edge_ref[f, d] = out_ref[f, d]
        return
    me = me_ref[0]
    row = lax.broadcasted_iota(jnp.int32, (SUBLANES, cells_x), 0)
    tail = jnp.zeros((SUBLANES, cells_x), jnp.float32)
    for i in range(lags_ref.shape[1]):
        tail = jnp.where(row == i, lags_ref[0, i].astype(jnp.float32), tail)
    for k, part_ref in enumerate(refs):
        d = row_y(jnp.bitwise_xor(me, k))
        for f in range(fields):
            part_ref[pl.ds(f * cells_z, cells_z)] = before_ref[f, d].astype(jnp.bfloat16)
            part_ref[pl.ds((fields + f) * cells_z, cells_z)] = out_ref[f, d].astype(jnp.bfloat16)
        part_ref[pl.ds(2 * fields * cells_z, SUBLANES)] = tail.astype(jnp.bfloat16)


def half_step(spec, side, extra, constant, levels, halo, groups):
    _, near, last = spec
    fields, planes, cells_z, cells_x = levels[0].shape[-4:]
    shape = jax.ShapeDtypeStruct
    full = shape((fields, planes, cells_z, cells_x), jnp.float32)
    outs, scratch = [full], []
    if near and last:
        rows = 2 * fields * cells_z + SUBLANES
        outs = [shape((rows, cells_x), jnp.bfloat16)] * groups
        scratch = [pltpu.VMEM(full.shape, full.dtype)]
    elif near:
        outs += [shape((fields, REACH, cells_z, cells_x), jnp.float32)]
    count = planes // 2
    cells = fields * count * cells_z * cells_x
    args = [side, *extra, *constant, *levels, *halo]
    scalars = 1 + len(extra)

    def kernel(*refs):
        if near and last:
            ins, refs = refs[: len(args)], refs[len(args) :]
            refs = (*ins, refs[groups], *refs[:groups], *refs[groups + 1 :])
        half_kernel(spec, *refs)

    return pl.pallas_call(
        kernel,
        out_shape=outs,
        in_specs=[SMEM] * scalars + [VMEM] * (len(args) - scalars),
        out_specs=[VMEM] * len(outs),
        scratch_shapes=[
            *scratch,
            pltpu.VMEM(
                (fields, count, cells_x // LANES, cells_z + 2 * SUBLANES, LANES), jnp.float32
            ),
            pltpu.VMEM((fields * count * cells_z, 3 * cells_x), jnp.bfloat16),
            pltpu.VMEM((fields * count * cells_z, cells_x), jnp.float32),
        ],
        compiler_params=pltpu.CompilerParams(vmem_limit_bytes=8 * 1024 * 1024),
        cost_estimate=pl.CostEstimate(
            flops=2000 * cells, bytes_accessed=16 * cells, transcendentals=0
        ),
        name="near" if near else "far",
    )(*args)


def turned_x(tiles, step, lane):
    count = len(tiles)
    if step == 0:
        return tiles
    if step > 0:
        rolled = [pltpu.roll(t, LANES - step, 1) for t in tiles]
        keep = lane < LANES - step
        return [jnp.where(keep, rolled[i], rolled[(i + 1) % count]) for i in range(count)]
    rolled = [pltpu.roll(t, -step, 1) for t in tiles]
    keep = lane >= -step
    return [jnp.where(keep, rolled[i], rolled[i - 1]) for i in range(count)]


FINE = 4


def image_kernel(spec, valid_ref, *refs):
    ours, groups, snaps, fields, start, finish = spec
    refs = list(refs)
    parts = [refs.pop(0) for _ in ours]
    before = None if start else refs.pop(0)
    tails = [refs.pop(0) for _ in range(groups)] if finish else []
    held, coarse, fine = refs[-3:]
    refs = refs[:-3]
    image = refs.pop() if finish else refs.pop(0)
    outs = refs
    offsets, cells_z, cells_x = image.shape
    half = offsets // 2
    tail = snaps * fields * cells_z
    place = 0
    for k, part in zip(ours, parts):

        @pl.when(valid_ref[k] > 0)
        def _(part=part, place=place):
            for i in range(snaps * fields):
                held[place, i] = part[pl.ds(i * cells_z, cells_z)].astype(jnp.float32)

        place = place + valid_ref[k]
    tiles_x = cells_x // LANES
    rows = 2 * SUBLANES
    lane = lax.broadcasted_iota(jnp.int32, (rows, LANES), 1)
    join = lambda tiles: jnp.concatenate(tiles, axis=1)
    cut = lambda value: [value[:, t * LANES : (t + 1) * LANES] for t in range(tiles_x)]

    for h in range(offsets):
        image[h] = jnp.zeros((cells_z, cells_x), jnp.float32) if start else before[h]

    def one(j, carry):
        shot, z = j // (cells_z // rows), lax.rem(j, cells_z // rows)
        at = pl.ds(pl.multiple_of(z * rows, rows), rows)
        for m in range(snaps):
            receiver = cut(held[shot, m * fields + 1, at])
            for b in range(offsets // FINE):
                coarse[m, b] = join(turned_x(receiver, FINE * b - half, lane))
            source = cut(held[shot, m * fields, at])
            for a in range(FINE):
                fine[m, a] = join(turned_x(source, -a, lane))
        for a in range(FINE):
            for b in range(offsets // FINE):
                total = image[FINE * b + a, at]
                for m in range(snaps):
                    total += fine[m, a] * coarse[m, b]
                image[FINE * b + a, at] = total
        return carry

    lax.fori_loop(0, place * (cells_z // rows), one, 0)
    if not finish:
        return
    lane = lax.broadcasted_iota(jnp.int32, (cells_z, LANES), 1)
    for k, out in enumerate(outs):
        ends = tails[k][pl.ds(tail, SUBLANES)].astype(jnp.float32)
        for i in range(out.shape[0]):
            lag = ends[i, 0].astype(jnp.int32)
            place = half + lag
            back = lax.rem(place, FINE)
            tiles = [image[place, :, pl.ds(t * LANES, LANES)] for t in range(tiles_x)]
            rolled = [pltpu.roll(tile, lax.rem(LANES - back, LANES), 1) for tile in tiles]
            keep = lane < LANES - back
            for t in range(tiles_x):
                x = lane + (t * LANES + lag)
                value = jnp.where(keep, rolled[t], rolled[(t + 1) % tiles_x])
                value = jnp.where((x >= 0) & (x < cells_x), value, 0.0)
                out[i, :, pl.ds(t * LANES, LANES)] = value.astype(out.dtype)


def imaged(spec, valid, parts, before, offsets):
    ours, groups, snaps, fields, start, finish = spec
    rows, cells_x = parts[0].shape
    cells_z = (rows - SUBLANES) // (snaps * fields)
    shape = jax.ShapeDtypeStruct
    if finish:
        per_group = offsets // groups
        outs = [shape((per_group, cells_z, cells_x), jnp.bfloat16)] * groups
        outs[0] = shape((per_group, cells_z, cells_x), jnp.float32)
    else:
        outs = [shape((offsets, cells_z, cells_x), jnp.float32)]
    args = [valid, *[parts[k] for k in ours]]
    args += [] if start else [before]
    args += [parts[k] for k in range(groups)] if finish else []
    scratch = [pltpu.VMEM((offsets, cells_z, cells_x), jnp.float32)] if finish else []
    strip = (2 * SUBLANES, cells_x)
    made = pl.pallas_call(
        functools.partial(image_kernel, spec),
        out_shape=outs,
        in_specs=[SMEM] + [VMEM] * (len(args) - 1),
        out_specs=[VMEM] * len(outs),
        scratch_shapes=[
            *scratch,
            pltpu.VMEM((len(ours), snaps * fields, cells_z, cells_x), jnp.float32),
            pltpu.VMEM((snaps, offsets // FINE, *strip), jnp.float32),
            pltpu.VMEM((snaps, FINE, *strip), jnp.float32),
        ],
        compiler_params=pltpu.CompilerParams(vmem_limit_bytes=8 * 1024 * 1024),
        cost_estimate=pl.CostEstimate(
            flops=200 * snaps * len(ours) * offsets * cells_z * cells_x,
            bytes_accessed=8 * offsets * cells_z * cells_x,
            transcendentals=0,
        ),
        name="image",
    )(*args)
    return made if finish else made[0]


def gather_kernel(me_ref, *refs):
    out_ref = refs[-1]
    for k, part_ref in enumerate(refs[:-1]):
        y = jnp.bitwise_xor(me_ref[0], k)
        for i in range(out_ref.shape[0]):
            out_ref[i, y] = part_ref[i].astype(jnp.float32)


def far_first(groups):
    order = (4, 5, 7, 3, 6, 2, 1)
    return [k for k in order if k < groups] + [k for k in range(8, groups)]


def on_device_planes(checkpoint, traces, courant_sq, holder, offset_lags):
    start = checkpoint[0]
    fields, planes, cells_z, cells_x = start.shape[1:]
    step_count = traces.shape[1]
    groups = lax.axis_size("off")
    per_group = offset_lags.shape[1]
    snaps = step_count // 2
    me = lax.axis_index("off").astype(jnp.int32)
    side = lax.axis_index("gy").astype(jnp.int32)
    slots = jnp.bitwise_xor(me, jnp.arange(groups, dtype=jnp.int32))
    valid = jnp.any(holder[None, :] == slots[:, None], axis=1).astype(jnp.int32)
    side1, me1 = side.reshape(1), me.reshape(1)
    swap = [(0, 1), (1, 0)]

    apart = jnp.abs(
        lax.broadcasted_iota(jnp.int32, (cells_x, cells_x), 0)
        - lax.broadcasted_iota(jnp.int32, (cells_x, cells_x), 1)
    )
    band = jnp.zeros((cells_x, cells_x), jnp.float32)
    for tap in range(1, REACH + 1):
        band = jnp.where(apart == tap, TAPS[tap], band)
    band = band.astype(jnp.bfloat16)

    edge = lax.dynamic_slice(
        checkpoint,
        (0, 1, 0, (1 - side) * (planes - REACH), 0, 0),
        (1, 1, fields, REACH, cells_z, cells_x),
    )[0, 0]
    earlier = current = None
    constant = [courant_sq, traces[0], band]
    for n in range(step_count):
        halo = lax.ppermute(edge, "gy", swap)
        last = n == step_count - 1
        levels = [start] if n == 0 else [start, current] if n == 1 else [earlier, current]
        fresh = half_step((n, False, last), side1, [], constant, levels, [], groups)[0]
        extra = [me1, offset_lags] if last else []
        made = half_step(
            (n, True, last), side1, extra, constant, levels, [halo, fresh], groups
        )
        if not last:
            earlier, (current, edge) = current, made
    parts = made

    def pairs(k):
        return [(i, i ^ k) for i in range(groups)]

    order = far_first(groups)
    got, back = {0: parts[0]}, {}
    for k in order:
        got[k] = lax.ppermute(parts[k], "off", pairs(k))
    offsets = groups * per_group
    stages = ((0, 4, 7, 6), (5, 3, 2, 1))
    images = None
    for i, ours in enumerate(stages):
        spec = (ours, groups, snaps, fields, i == 0, i == len(stages) - 1)
        images = imaged(spec, valid, got, images, offsets)
    for k in order:
        back[k] = lax.ppermute(images[k], "off", pairs(k))
    back[0] = images[0]
    return pl.pallas_call(
        gather_kernel,
        out_shape=jax.ShapeDtypeStruct((per_group, planes, cells_z, cells_x), jnp.float32),
        in_specs=[SMEM] + [VMEM] * groups,
        out_specs=VMEM,
        compiler_params=pltpu.CompilerParams(vmem_limit_bytes=8 * 1024 * 1024),
        name="gather",
    )(me1, *[back[k] for k in range(groups)])


def solution(mesh):
    placed = (
        P(("survey", "off"), None, None, "gy", None, None),
        P(("survey", "off"), None, "gy", None),
        P("gy", None, None),
        P("survey"),
        P(("survey", "off"), None),
    )

    def on_device(checkpoint, traces, courant_sq, holder, offset_lags):
        groups, sides = mesh.shape["off"], mesh.shape["gy"]
        planes, cells_z, cells_x = courant_sq.shape
        fits = (
            groups == planes
            and groups & (groups - 1) == 0
            and sides == 2
            and planes == 2 * REACH
            and cells_z % (2 * SUBLANES) == 0
            and cells_x % LANES == 0
            and cells_x >= 2 * LANES
            and traces.shape[1] == 4
            and groups * offset_lags.shape[1] <= LANES
            and offset_lags.shape[1] <= SUBLANES
        )
        chosen = on_device_planes if fits else on_device_general
        return chosen(checkpoint, traces, courant_sq, holder, offset_lags)

    return jax.shard_map(
        on_device,
        mesh=mesh,
        in_specs=placed,
        out_specs=P(("survey", "off"), "gy", None, None),
        check_vma=False,
    )
```

```python
import functools
import jax
import jax.numpy as jnp
from jax import lax
from jax.experimental import pallas as pl
from jax.experimental.pallas import tpu as pltpu
from jax.sharding import PartitionSpec as P

stencil_taps = (-205.0 / 72.0, 8.0 / 5.0, -1.0 / 5.0, 8.0 / 315.0, -1.0 / 560.0)
REACH = 4
COMMON, BAND_UNIT = 5040.0, 4096.0
TAPS = tuple(round(tap * COMMON) / BAND_UNIT for tap in stencil_taps)
LANES = 128
SUBLANES = 8
VMEM = pl.BlockSpec(memory_space=pltpu.VMEM)
SMEM = pl.BlockSpec(memory_space=pltpu.SMEM)


def extended_2(shard, sides, width):
    for axis, dim in sides:
        devices, length = (lax.axis_size(axis), shard.shape[dim])
        up = [(i, (i + 1) % devices) for i in range(devices - 1)]
        down = [(j, i) for i, j in up]
        last = lax.slice_in_dim(shard, length - width, length, axis=dim)
        initial = lax.slice_in_dim(shard, 0, width, axis=dim)
        before = lax.ppermute(last, axis, up)
        after = lax.ppermute(initial, axis, down)
        shard = jnp.concatenate([before, shard, after], axis=dim)
    return shard


def spread(value, axis, source):
    kept = jnp.where(lax.axis_index(axis) == source, value, 0).astype(value.dtype)
    return lax.psum(kept, axis)


def laplace(extended):
    cells_y = extended.shape[-3] - 8
    cells_z = extended.shape[-2]
    cells_x = extended.shape[-1]
    leading = [(0, 0)] * (extended.ndim - 2)
    padded = jnp.pad(extended, leading + [(4, 4), (4, 4)])

    def shifted(step_y, step_z, step_x):
        return padded[
            ...,
            4 + step_y : 4 + step_y + cells_y,
            4 + step_z : 4 + step_z + cells_z,
            4 + step_x : 4 + step_x + cells_x,
        ]

    summed = 3.0 * stencil_taps[0] * shifted(0, 0, 0)
    for tap_no in range(1, 5):
        beside_all = shifted(tap_no, 0, 0) + shifted(-tap_no, 0, 0)
        beside_all = beside_all + shifted(0, tap_no, 0) + shifted(0, -tap_no, 0)
        beside_all = beside_all + shifted(0, 0, tap_no) + shifted(0, 0, -tap_no)
        summed = summed + stencil_taps[tap_no] * beside_all
    return summed


def propagate_step(earlier, current, courant_sq, drive):
    extended = extended_2(current, (("gy", 2),), 4)
    advanced = 2.0 * current - earlier + courant_sq * laplace(extended)
    advanced = advanced.at[:, 1, :, 0, :].add(drive)
    return (current, advanced)


def correlate(image_acc, source, receiver, my_lags, half_span):
    cells_x = receiver.shape[-1]
    padded = jnp.pad(receiver, ((0, 0), (0, 0), (half_span, half_span)))
    moved = jax.vmap(
        lambda lag_value: lax.dynamic_slice_in_dim(padded, half_span + lag_value, cells_x, 2)
    )(my_lags)
    return image_acc + source.astype(jnp.float32)[None] * moved.astype(jnp.float32)


def on_device_general(checkpoint, traces, courant_sq, holder, offset_lags):
    shot_count = holder.shape[0]
    step_count = traces.shape[1]
    my_lags = offset_lags[0]
    half_span = lax.axis_size("off") * offset_lags.shape[1] // 2
    image_acc = jnp.zeros((offset_lags.shape[1],) + courant_sq.shape, jnp.float32)
    earlier = checkpoint[:, 0]
    current = checkpoint[:, 1]
    collected = []
    for step_no in range(step_count):
        earlier, current = propagate_step(earlier, current, courant_sq, traces[:, step_no])
        if step_no % 2 == 1:
            snapshot = current[0].astype(jnp.bfloat16)
            collected.append(snapshot)
    snap_runs = jnp.stack(collected)
    for shot_no in range(shot_count):
        received = spread(snap_runs, "off", holder[shot_no])
        for snap_no in range(received.shape[0]):
            image_acc = correlate(
                image_acc, received[snap_no, 0], received[snap_no, 1], my_lags, half_span
            )
    return image_acc


def half_kernel(spec, *refs):
    step_no, near, last = spec
    refs = list(refs)
    side = refs.pop(0)[0]
    if last and near:
        me_ref, lags_ref = refs.pop(0), refs.pop(0)
    courant_ref, drive_ref, band_ref = refs.pop(0), refs.pop(0), refs.pop(0)
    start_ref = refs.pop(0) if step_no < 2 else None
    before_ref = refs.pop(0) if step_no >= 2 else None
    current_ref = refs.pop(0) if step_no >= 1 else None
    halo_ref = refs.pop(0) if near else None
    fresh_ref = refs.pop(0) if near else None
    along_x, split, ext = refs.pop(), refs.pop(), refs.pop()
    out_ref = refs.pop(0)
    fields, planes, cells_z, cells_x = out_ref.shape
    count = planes // 2
    tiles_x = cells_x // LANES
    everything = slice(None)

    def row_y(d):
        return jnp.where(side == 0, planes - 1 - d, d)

    def current(f, d, at=()):
        if d < 0:
            j = -1 - d
            if step_no == 0:
                j = jnp.where(side == 0, j, REACH - 1 - j)
            return halo_ref[(f, j, *at)]
        if step_no == 0:
            return start_ref[(1, f, row_y(d), *at)]
        return current_ref[(f, d, *at)]

    def before(f, d, at=()):
        if step_no < 2:
            return start_ref[(step_no, f, row_y(d), *at)]
        return before_ref[(f, d, *at)]

    base = 0 if near else count
    pad = jnp.zeros((SUBLANES, LANES), jnp.float32)
    for f in range(fields):
        for i in range(count):
            here = current(f, base + i)
            for t in range(tiles_x):
                ext[f, i, t, pl.ds(0, SUBLANES)] = pad
                ext[f, i, t, pl.ds(SUBLANES, cells_z)] = here[:, t * LANES : (t + 1) * LANES]
                ext[f, i, t, pl.ds(SUBLANES + cells_z, SUBLANES)] = pad
            high = here.astype(jnp.bfloat16)
            left = here - high.astype(jnp.float32)
            middle = left.astype(jnp.bfloat16)
            low = (left - middle.astype(jnp.float32)).astype(jnp.bfloat16)
            at = pl.ds((f * count + i) * cells_z, cells_z)
            for j, piece in enumerate((high, middle, low)):
                split[at, pl.ds(j * cells_x, cells_x)] = piece
    band = band_ref[...]
    along_x[...] = jnp.dot(
        split[...], jnp.concatenate([band] * 3, axis=0), preferred_element_type=jnp.float32
    )
    for i in range(count):
        d = base + i
        y = row_y(d)
        for t in range(tiles_x):
            across = pl.ds(t * LANES, LANES)
            at = (everything, across)
            courant = courant_ref[y, :, across]
            for f in range(fields):
                here = ext[f, i, t, pl.ds(SUBLANES, cells_z)]
                lap = (3.0 * TAPS[0]) * here
                lap += along_x[pl.ds((f * count + i) * cells_z, cells_z), across]
                for tap in range(1, REACH + 1):
                    beside = (
                        ext[f, i, t, pl.ds(SUBLANES + tap, cells_z)]
                        + ext[f, i, t, pl.ds(SUBLANES - tap, cells_z)]
                    )
                    for other in (d - tap, d + tap):
                        if other < planes:
                            beside += current(f, other, at)
                    lap += TAPS[tap] * beside
                out_ref[f, d, :, across] = (2.0 * here - before(f, d, at)) + courant * lap
        out_ref[1, d, pl.ds(0, 1)] = (
            out_ref[1, d, pl.ds(0, 1)] + drive_ref[step_no, pl.ds(y, 1)]
        )
    if not near:
        return
    for f in range(fields):
        for d in range(count, planes):
            out_ref[f, d] = fresh_ref[f, d]
    if not last:
        edge_ref = refs.pop(0)
        for f in range(fields):
            for d in range(REACH):
                edge_ref[f, d] = out_ref[f, d]
        return
    me = me_ref[0]
    row = lax.broadcasted_iota(jnp.int32, (SUBLANES, cells_x), 0)
    tail = jnp.zeros((SUBLANES, cells_x), jnp.float32)
    for i in range(lags_ref.shape[1]):
        tail = jnp.where(row == i, lags_ref[0, i].astype(jnp.float32), tail)
    for k, part_ref in enumerate(refs):
        d = row_y(jnp.bitwise_xor(me, k))
        for f in range(fields):
            part_ref[pl.ds(f * cells_z, cells_z)] = before_ref[f, d].astype(jnp.bfloat16)
            part_ref[pl.ds((fields + f) * cells_z, cells_z)] = out_ref[f, d].astype(jnp.bfloat16)
        part_ref[pl.ds(2 * fields * cells_z, SUBLANES)] = tail.astype(jnp.bfloat16)


def half_step(spec, side, extra, constant, levels, halo, groups):
    _, near, last = spec
    fields, planes, cells_z, cells_x = levels[0].shape[-4:]
    shape = jax.ShapeDtypeStruct
    full = shape((fields, planes, cells_z, cells_x), jnp.float32)
    outs, scratch = [full], []
    if near and last:
        rows = 2 * fields * cells_z + SUBLANES
        outs = [shape((rows, cells_x), jnp.bfloat16)] * groups
        scratch = [pltpu.VMEM(full.shape, full.dtype)]
    elif near:
        outs += [shape((fields, REACH, cells_z, cells_x), jnp.float32)]
    count = planes // 2
    cells = fields * count * cells_z * cells_x
    args = [side, *extra, *constant, *levels, *halo]
    scalars = 1 + len(extra)

    def kernel(*refs):
        if near and last:
            ins, refs = refs[: len(args)], refs[len(args) :]
            refs = (*ins, refs[groups], *refs[:groups], *refs[groups + 1 :])
        half_kernel(spec, *refs)

    return pl.pallas_call(
        kernel,
        out_shape=outs,
        in_specs=[SMEM] * scalars + [VMEM] * (len(args) - scalars),
        out_specs=[VMEM] * len(outs),
        scratch_shapes=[
            *scratch,
            pltpu.VMEM(
                (fields, count, cells_x // LANES, cells_z + 2 * SUBLANES, LANES), jnp.float32
            ),
            pltpu.VMEM((fields * count * cells_z, 3 * cells_x), jnp.bfloat16),
            pltpu.VMEM((fields * count * cells_z, cells_x), jnp.float32),
        ],
        compiler_params=pltpu.CompilerParams(vmem_limit_bytes=8 * 1024 * 1024),
        cost_estimate=pl.CostEstimate(
            flops=2000 * cells, bytes_accessed=16 * cells, transcendentals=0
        ),
        name="near" if near else "far",
    )(*args)


def turned_x(tiles, step, lane):
    count = len(tiles)
    if step == 0:
        return tiles
    if step > 0:
        rolled = [pltpu.roll(t, LANES - step, 1) for t in tiles]
        keep = lane < LANES - step
        return [jnp.where(keep, rolled[i], rolled[(i + 1) % count]) for i in range(count)]
    rolled = [pltpu.roll(t, -step, 1) for t in tiles]
    keep = lane >= -step
    return [jnp.where(keep, rolled[i], rolled[i - 1]) for i in range(count)]


FINE = 4


def image_kernel(spec, valid_ref, *refs):
    ours, groups, snaps, fields, start, finish = spec
    refs = list(refs)
    parts = [refs.pop(0) for _ in ours]
    before = None if start else refs.pop(0)
    tails = [refs.pop(0) for _ in range(groups)] if finish else []
    held, coarse, fine = refs[-3:]
    refs = refs[:-3]
    image = refs.pop() if finish else refs.pop(0)
    outs = refs
    offsets, cells_z, cells_x = image.shape
    half = offsets // 2
    tail = snaps * fields * cells_z
    place = 0
    for k, part in zip(ours, parts):

        @pl.when(valid_ref[k] > 0)
        def _(part=part, place=place):
            for i in range(snaps * fields):
                held[place, i] = part[pl.ds(i * cells_z, cells_z)].astype(jnp.float32)

        place = place + valid_ref[k]
    tiles_x = cells_x // LANES
    rows = 2 * SUBLANES
    lane = lax.broadcasted_iota(jnp.int32, (rows, LANES), 1)
    join = lambda tiles: jnp.concatenate(tiles, axis=1)
    cut = lambda value: [value[:, t * LANES : (t + 1) * LANES] for t in range(tiles_x)]

    for h in range(offsets):
        image[h] = jnp.zeros((cells_z, cells_x), jnp.float32) if start else before[h]

    def one(j, carry):
        shot, z = j // (cells_z // rows), lax.rem(j, cells_z // rows)
        at = pl.ds(pl.multiple_of(z * rows, rows), rows)
        for m in range(snaps):
            receiver = cut(held[shot, m * fields + 1, at])
            for b in range(offsets // FINE):
                coarse[m, b] = join(turned_x(receiver, FINE * b - half, lane))
            source = cut(held[shot, m * fields, at])
            for a in range(FINE):
                fine[m, a] = join(turned_x(source, -a, lane))
        for a in range(FINE):
            for b in range(offsets // FINE):
                total = image[FINE * b + a, at]
                for m in range(snaps):
                    total += fine[m, a] * coarse[m, b]
                image[FINE * b + a, at] = total
        return carry

    lax.fori_loop(0, place * (cells_z // rows), one, 0)
    if not finish:
        return
    lane = lax.broadcasted_iota(jnp.int32, (cells_z, LANES), 1)
    for k, out in enumerate(outs):
        ends = tails[k][pl.ds(tail, SUBLANES)].astype(jnp.float32)
        for i in range(out.shape[0]):
            lag = ends[i, 0].astype(jnp.int32)
            place = half + lag
            back = lax.rem(place, FINE)
            tiles = [image[place, :, pl.ds(t * LANES, LANES)] for t in range(tiles_x)]
            rolled = [pltpu.roll(tile, lax.rem(LANES - back, LANES), 1) for tile in tiles]
            keep = lane < LANES - back
            for t in range(tiles_x):
                x = lane + (t * LANES + lag)
                value = jnp.where(keep, rolled[t], rolled[(t + 1) % tiles_x])
                value = jnp.where((x >= 0) & (x < cells_x), value, 0.0)
                out[i, :, pl.ds(t * LANES, LANES)] = value.astype(out.dtype)


def imaged(spec, valid, parts, before, offsets):
    ours, groups, snaps, fields, start, finish = spec
    rows, cells_x = parts[0].shape
    cells_z = (rows - SUBLANES) // (snaps * fields)
    shape = jax.ShapeDtypeStruct
    if finish:
        per_group = offsets // groups
        outs = [shape((per_group, cells_z, cells_x), jnp.bfloat16)] * groups
        outs[0] = shape((per_group, cells_z, cells_x), jnp.float32)
    else:
        outs = [shape((offsets, cells_z, cells_x), jnp.float32)]
    args = [valid, *[parts[k] for k in ours]]
    args += [] if start else [before]
    args += [parts[k] for k in range(groups)] if finish else []
    scratch = [pltpu.VMEM((offsets, cells_z, cells_x), jnp.float32)] if finish else []
    strip = (2 * SUBLANES, cells_x)
    made = pl.pallas_call(
        functools.partial(image_kernel, spec),
        out_shape=outs,
        in_specs=[SMEM] + [VMEM] * (len(args) - 1),
        out_specs=[VMEM] * len(outs),
        scratch_shapes=[
            *scratch,
            pltpu.VMEM((len(ours), snaps * fields, cells_z, cells_x), jnp.float32),
            pltpu.VMEM((snaps, offsets // FINE, *strip), jnp.float32),
            pltpu.VMEM((snaps, FINE, *strip), jnp.float32),
        ],
        compiler_params=pltpu.CompilerParams(vmem_limit_bytes=8 * 1024 * 1024),
        cost_estimate=pl.CostEstimate(
            flops=200 * snaps * len(ours) * offsets * cells_z * cells_x,
            bytes_accessed=8 * offsets * cells_z * cells_x,
            transcendentals=0,
        ),
        name="image",
    )(*args)
    return made if finish else made[0]


def gather_kernel(me_ref, *refs):
    out_ref = refs[-1]
    for k, part_ref in enumerate(refs[:-1]):
        y = jnp.bitwise_xor(me_ref[0], k)
        for i in range(out_ref.shape[0]):
            out_ref[i, y] = part_ref[i].astype(jnp.float32)


def far_first(groups):
    order = (6, 7, 5, 4, 2, 3, 1)
    return [k for k in order if k < groups] + [k for k in range(8, groups)]


def on_device_planes(checkpoint, traces, courant_sq, holder, offset_lags):
    start = checkpoint[0]
    fields, planes, cells_z, cells_x = start.shape[1:]
    step_count = traces.shape[1]
    groups = lax.axis_size("off")
    per_group = offset_lags.shape[1]
    snaps = step_count // 2
    me = lax.axis_index("off").astype(jnp.int32)
    side = lax.axis_index("gy").astype(jnp.int32)
    slots = jnp.bitwise_xor(me, jnp.arange(groups, dtype=jnp.int32))
    valid = jnp.any(holder[None, :] == slots[:, None], axis=1).astype(jnp.int32)
    side1, me1 = side.reshape(1), me.reshape(1)
    swap = [(0, 1), (1, 0)]

    apart = jnp.abs(
        lax.broadcasted_iota(jnp.int32, (cells_x, cells_x), 0)
        - lax.broadcasted_iota(jnp.int32, (cells_x, cells_x), 1)
    )
    band = jnp.zeros((cells_x, cells_x), jnp.float32)
    for tap in range(1, REACH + 1):
        band = jnp.where(apart == tap, TAPS[tap], band)
    band = band.astype(jnp.bfloat16)

    edge = lax.dynamic_slice(
        checkpoint,
        (0, 1, 0, (1 - side) * (planes - REACH), 0, 0),
        (1, 1, fields, REACH, cells_z, cells_x),
    )[0, 0]
    earlier = current = None
    drive = jnp.where(side >= 0, traces[0], 0.0)
    constant = [courant_sq * (BAND_UNIT / COMMON), drive, band]
    for n in range(step_count):
        halo = lax.ppermute(edge, "gy", swap)
        last = n == step_count - 1
        levels = [start] if n == 0 else [start, current] if n == 1 else [earlier, current]
        fresh = half_step((n, False, last), side1, [], constant, levels, [], groups)[0]
        extra = [me1, offset_lags] if last else []
        made = half_step(
            (n, True, last), side1, extra, constant, levels, [halo, fresh], groups
        )
        if not last:
            earlier, (current, edge) = current, made
    parts = made

    def pairs(k):
        return [(i, i ^ k) for i in range(groups)]

    order = far_first(groups)
    got, back = {0: parts[0]}, {}
    for k in order:
        got[k] = lax.ppermute(parts[k], "off", pairs(k))
    offsets = groups * per_group
    stages = ((0, 6, 7, 1, 2), (5, 4, 3))
    images = None
    for i, ours in enumerate(stages):
        spec = (ours, groups, snaps, fields, i == 0, i == len(stages) - 1)
        images = imaged(spec, valid, got, images, offsets)
    for k in order:
        back[k] = lax.ppermute(images[k], "off", pairs(k))
    back[0] = images[0]
    return pl.pallas_call(
        gather_kernel,
        out_shape=jax.ShapeDtypeStruct((per_group, planes, cells_z, cells_x), jnp.float32),
        in_specs=[SMEM] + [VMEM] * groups,
        out_specs=VMEM,
        compiler_params=pltpu.CompilerParams(vmem_limit_bytes=8 * 1024 * 1024),
        name="gather",
    )(me1, *[back[k] for k in range(groups)])


def solution(mesh):
    placed = (
        P(("survey", "off"), None, None, "gy", None, None),
        P(("survey", "off"), None, "gy", None),
        P("gy", None, None),
        P("survey"),
        P(("survey", "off"), None),
    )

    def on_device(checkpoint, traces, courant_sq, holder, offset_lags):
        groups, sides = mesh.shape["off"], mesh.shape["gy"]
        planes, cells_z, cells_x = courant_sq.shape
        fits = (
            groups == planes
            and groups & (groups - 1) == 0
            and sides == 2
            and planes == 2 * REACH
            and cells_z % (2 * SUBLANES) == 0
            and cells_x % LANES == 0
            and cells_x >= 2 * LANES
            and traces.shape[1] == 4
            and groups * offset_lags.shape[1] <= LANES
            and offset_lags.shape[1] <= SUBLANES
        )
        chosen = on_device_planes if fits else on_device_general
        return chosen(checkpoint, traces, courant_sq, holder, offset_lags)

    return jax.shard_map(
        on_device,
        mesh=mesh,
        in_specs=placed,
        out_specs=P(("survey", "off"), "gy", None, None),
        check_vma=False,
    )
```

```python
import functools
import jax
import jax.numpy as jnp
from jax import lax
from jax.experimental import pallas as pl
from jax.experimental.pallas import tpu as pltpu
from jax.sharding import PartitionSpec as P

stencil_taps = (-205.0 / 72.0, 8.0 / 5.0, -1.0 / 5.0, 8.0 / 315.0, -1.0 / 560.0)
REACH = 4
COMMON, BAND_UNIT = 5040.0, 4096.0
TAPS = tuple(round(tap * COMMON) / BAND_UNIT for tap in stencil_taps)
LANES = 128
SUBLANES = 8
VMEM = pl.BlockSpec(memory_space=pltpu.VMEM)
SMEM = pl.BlockSpec(memory_space=pltpu.SMEM)


def extended_2(shard, sides, width):
    for axis, dim in sides:
        devices, length = (lax.axis_size(axis), shard.shape[dim])
        up = [(i, (i + 1) % devices) for i in range(devices - 1)]
        down = [(j, i) for i, j in up]
        last = lax.slice_in_dim(shard, length - width, length, axis=dim)
        initial = lax.slice_in_dim(shard, 0, width, axis=dim)
        before = lax.ppermute(last, axis, up)
        after = lax.ppermute(initial, axis, down)
        shard = jnp.concatenate([before, shard, after], axis=dim)
    return shard


def spread(value, axis, source):
    kept = jnp.where(lax.axis_index(axis) == source, value, 0).astype(value.dtype)
    return lax.psum(kept, axis)


def laplace(extended):
    cells_y = extended.shape[-3] - 8
    cells_z = extended.shape[-2]
    cells_x = extended.shape[-1]
    leading = [(0, 0)] * (extended.ndim - 2)
    padded = jnp.pad(extended, leading + [(4, 4), (4, 4)])

    def shifted(step_y, step_z, step_x):
        return padded[
            ...,
            4 + step_y : 4 + step_y + cells_y,
            4 + step_z : 4 + step_z + cells_z,
            4 + step_x : 4 + step_x + cells_x,
        ]

    summed = 3.0 * stencil_taps[0] * shifted(0, 0, 0)
    for tap_no in range(1, 5):
        beside_all = shifted(tap_no, 0, 0) + shifted(-tap_no, 0, 0)
        beside_all = beside_all + shifted(0, tap_no, 0) + shifted(0, -tap_no, 0)
        beside_all = beside_all + shifted(0, 0, tap_no) + shifted(0, 0, -tap_no)
        summed = summed + stencil_taps[tap_no] * beside_all
    return summed


def propagate_step(earlier, current, courant_sq, drive):
    extended = extended_2(current, (("gy", 2),), 4)
    advanced = 2.0 * current - earlier + courant_sq * laplace(extended)
    advanced = advanced.at[:, 1, :, 0, :].add(drive)
    return (current, advanced)


def correlate(image_acc, source, receiver, my_lags, half_span):
    cells_x = receiver.shape[-1]
    padded = jnp.pad(receiver, ((0, 0), (0, 0), (half_span, half_span)))
    moved = jax.vmap(
        lambda lag_value: lax.dynamic_slice_in_dim(padded, half_span + lag_value, cells_x, 2)
    )(my_lags)
    return image_acc + source.astype(jnp.float32)[None] * moved.astype(jnp.float32)


def on_device_general(checkpoint, traces, courant_sq, holder, offset_lags):
    shot_count = holder.shape[0]
    step_count = traces.shape[1]
    my_lags = offset_lags[0]
    half_span = lax.axis_size("off") * offset_lags.shape[1] // 2
    image_acc = jnp.zeros((offset_lags.shape[1],) + courant_sq.shape, jnp.float32)
    earlier = checkpoint[:, 0]
    current = checkpoint[:, 1]
    collected = []
    for step_no in range(step_count):
        earlier, current = propagate_step(earlier, current, courant_sq, traces[:, step_no])
        if step_no % 2 == 1:
            snapshot = current[0].astype(jnp.bfloat16)
            collected.append(snapshot)
    snap_runs = jnp.stack(collected)
    for shot_no in range(shot_count):
        received = spread(snap_runs, "off", holder[shot_no])
        for snap_no in range(received.shape[0]):
            image_acc = correlate(
                image_acc, received[snap_no, 0], received[snap_no, 1], my_lags, half_span
            )
    return image_acc


def half_kernel(spec, *refs):
    step_no, near, last = spec
    first_snap = near and step_no == 1
    refs = list(refs)
    side = refs.pop(0)[0]
    if first_snap or (last and near):
        me_ref, lags_ref = refs.pop(0), refs.pop(0)
    courant_ref, drive_ref, band_ref = refs.pop(0), refs.pop(0), refs.pop(0)
    start_ref = refs.pop(0) if step_no < 2 else None
    before_ref = refs.pop(0) if step_no >= 2 else None
    current_ref = refs.pop(0) if step_no >= 1 else None
    halo_ref = refs.pop(0) if near else None
    fresh_ref = refs.pop(0) if near else None
    along_x, split, ext = refs.pop(), refs.pop(), refs.pop()
    out_ref = refs.pop(0)
    fields, planes, cells_z, cells_x = out_ref.shape
    count = planes // 2
    tiles_x = cells_x // LANES
    everything = slice(None)

    def row_y(d):
        return jnp.where(side == 0, planes - 1 - d, d)

    def current(f, d, at=()):
        if d < 0:
            j = -1 - d
            if step_no == 0:
                j = jnp.where(side == 0, j, REACH - 1 - j)
            return halo_ref[(f, j, *at)]
        if step_no == 0:
            return start_ref[(1, f, row_y(d), *at)]
        return current_ref[(f, d, *at)]

    def before(f, d, at=()):
        if step_no < 2:
            return start_ref[(step_no, f, row_y(d), *at)]
        return before_ref[(f, d, *at)]

    base = 0 if near else count
    pad = jnp.zeros((SUBLANES, LANES), jnp.float32)
    for f in range(fields):
        for i in range(count):
            here = current(f, base + i)
            for t in range(tiles_x):
                ext[f, i, t, pl.ds(0, SUBLANES)] = pad
                ext[f, i, t, pl.ds(SUBLANES, cells_z)] = here[:, t * LANES : (t + 1) * LANES]
                ext[f, i, t, pl.ds(SUBLANES + cells_z, SUBLANES)] = pad
            high = here.astype(jnp.bfloat16)
            left = here - high.astype(jnp.float32)
            middle = left.astype(jnp.bfloat16)
            low = (left - middle.astype(jnp.float32)).astype(jnp.bfloat16)
            at = pl.ds((f * count + i) * cells_z, cells_z)
            for j, piece in enumerate((high, middle, low)):
                split[at, pl.ds(j * cells_x, cells_x)] = piece
    band = band_ref[...]
    along_x[...] = jnp.dot(
        split[...], jnp.concatenate([band] * 3, axis=0), preferred_element_type=jnp.float32
    )
    for i in range(count):
        d = base + i
        y = row_y(d)
        for t in range(tiles_x):
            across = pl.ds(t * LANES, LANES)
            at = (everything, across)
            courant = courant_ref[y, :, across]
            for f in range(fields):
                here = ext[f, i, t, pl.ds(SUBLANES, cells_z)]
                lap = (3.0 * TAPS[0]) * here
                lap += along_x[pl.ds((f * count + i) * cells_z, cells_z), across]
                for tap in range(1, REACH + 1):
                    beside = (
                        ext[f, i, t, pl.ds(SUBLANES + tap, cells_z)]
                        + ext[f, i, t, pl.ds(SUBLANES - tap, cells_z)]
                    )
                    for other in (d - tap, d + tap):
                        if other < planes:
                            beside += current(f, other, at)
                    lap += TAPS[tap] * beside
                out_ref[f, d, :, across] = (2.0 * here - before(f, d, at)) + courant * lap
        out_ref[1, d, pl.ds(0, 1)] = (
            out_ref[1, d, pl.ds(0, 1)] + drive_ref[step_no, pl.ds(y, 1)]
        )
    if not near:
        return
    for f in range(fields):
        for d in range(count, planes):
            out_ref[f, d] = fresh_ref[f, d]
    if not last:
        edge_ref = refs.pop(0)
        for f in range(fields):
            for d in range(REACH):
                edge_ref[f, d] = out_ref[f, d]
        if first_snap:
            for i, part_ref in enumerate(refs):
                for j in range(2):
                    d = row_y(jnp.bitwise_xor(me_ref[0], FAR[i] + j))
                    for f in range(fields):
                        at = pl.ds((j * fields + f) * cells_z, cells_z)
                        part_ref[at] = out_ref[f, d].astype(jnp.bfloat16)
        return
    me = me_ref[0]
    row = lax.broadcasted_iota(jnp.int32, (TAIL, cells_x), 0)
    tail = jnp.zeros((TAIL, cells_x), jnp.float32)
    for i in range(lags_ref.shape[1]):
        tail = jnp.where(row == i, lags_ref[0, i].astype(jnp.float32), tail)
    for k, part_ref in enumerate(refs):
        d = row_y(jnp.bitwise_xor(me, k))
        at = 0
        for levels in [before_ref, out_ref] if k < NEAR else [out_ref]:
            for f in range(fields):
                part_ref[pl.ds(at, cells_z)] = levels[f, d].astype(jnp.bfloat16)
                at += cells_z
        part_ref[pl.ds(at, TAIL)] = tail.astype(jnp.bfloat16)


def half_step(spec, side, extra, constant, levels, halo, groups):
    step_no, near, last = spec
    fields, planes, cells_z, cells_x = levels[0].shape[-4:]
    shape = jax.ShapeDtypeStruct
    full = shape((fields, planes, cells_z, cells_x), jnp.float32)
    outs, scratch = [full], []
    if near and last:
        outs = [
            shape(((2 if k < NEAR else 1) * fields * cells_z + TAIL, cells_x), jnp.bfloat16)
            for k in range(groups)
        ]
        scratch = [pltpu.VMEM(full.shape, full.dtype)]
    elif near:
        outs += [shape((fields, REACH, cells_z, cells_x), jnp.float32)]
    if near and step_no == 1:
        outs += [shape((2 * fields * cells_z, cells_x), jnp.bfloat16)] * len(FAR)
    count = planes // 2
    cells = fields * count * cells_z * cells_x
    args = [side, *extra, *constant, *levels, *halo]
    scalars = 1 + len(extra)

    def kernel(*refs):
        if near and last:
            ins, refs = refs[: len(args)], refs[len(args) :]
            refs = (*ins, refs[groups], *refs[:groups], *refs[groups + 1 :])
        half_kernel(spec, *refs)

    return pl.pallas_call(
        kernel,
        out_shape=outs,
        in_specs=[SMEM] * scalars + [VMEM] * (len(args) - scalars),
        out_specs=[VMEM] * len(outs),
        scratch_shapes=[
            *scratch,
            pltpu.VMEM(
                (fields, count, cells_x // LANES, cells_z + 2 * SUBLANES, LANES), jnp.float32
            ),
            pltpu.VMEM((fields * count * cells_z, 3 * cells_x), jnp.bfloat16),
            pltpu.VMEM((fields * count * cells_z, cells_x), jnp.float32),
        ],
        compiler_params=pltpu.CompilerParams(vmem_limit_bytes=8 * 1024 * 1024),
        cost_estimate=pl.CostEstimate(
            flops=2000 * cells, bytes_accessed=16 * cells, transcendentals=0
        ),
        name="near" if near else "far",
    )(*args)


def turned_x(tiles, step, lane):
    count = len(tiles)
    if step == 0:
        return tiles
    if step > 0:
        rolled = [pltpu.roll(t, LANES - step, 1) for t in tiles]
        keep = lane < LANES - step
        return [jnp.where(keep, rolled[i], rolled[(i + 1) % count]) for i in range(count)]
    rolled = [pltpu.roll(t, -step, 1) for t in tiles]
    keep = lane >= -step
    return [jnp.where(keep, rolled[i], rolled[i - 1]) for i in range(count)]


FINE = 4
NEAR, FAR = 4, (6, 4)
TAIL = 16


def relay_kernel(part_ref, *refs):
    *early, out_ref = refs
    rows = part_ref.shape[0]
    half = early[0].shape[0] // 2
    out_ref[pl.ds(0, rows)] = part_ref[...]
    for i, ref in enumerate(early):
        out_ref[pl.ds(rows + i * half, half)] = ref[pl.ds(half, half)]


def relayed(part, early):
    rows, cells_x = part.shape
    half = early[0].shape[0] // 2
    return pl.pallas_call(
        relay_kernel,
        out_shape=jax.ShapeDtypeStruct((rows + len(early) * half, cells_x), part.dtype),
        in_specs=[VMEM] * (1 + len(early)),
        out_specs=VMEM,
        compiler_params=pltpu.CompilerParams(vmem_limit_bytes=8 * 1024 * 1024),
        cost_estimate=pl.CostEstimate(
            flops=rows * cells_x, bytes_accessed=4 * rows * cells_x, transcendentals=0
        ),
        name="relay",
    )(part, *early)


def found_at(k, snaps, fields, cells_z):
    size = fields * cells_z
    if k < NEAR:
        return [(k, m * size) for m in range(snaps)]
    i = FAR.index(k - k % 2)
    if k % 2 == 0:
        return [(-1 - i, 0), (k, 0)]
    return [(1, 2 * size + TAIL + i * size), (k, 0)]


def image_kernel(spec, valid_ref, *refs):
    ours, groups, snaps, fields, start, finish = spec
    refs = list(refs)
    names = wanted(ours, groups, snaps, finish)
    arrays = {name: refs.pop(0) for name in names}
    before = None if start else refs.pop(0)
    held, coarse, fine = refs[-3:]
    refs = refs[:-3]
    image = refs.pop() if finish else refs.pop(0)
    outs = refs
    offsets, cells_z, cells_x = image.shape
    half = offsets // 2
    place = 0
    for k in ours:

        @pl.when(valid_ref[k] > 0)
        def _(k=k, place=place):
            for m, (name, row) in enumerate(found_at(k, snaps, fields, cells_z)):
                for f in range(fields):
                    value = arrays[name][pl.ds(row + f * cells_z, cells_z)]
                    held[place, m * fields + f] = value.astype(jnp.float32)

        place = place + valid_ref[k]
    tiles_x = cells_x // LANES
    rows = 2 * SUBLANES
    lane = lax.broadcasted_iota(jnp.int32, (rows, LANES), 1)
    join = lambda tiles: jnp.concatenate(tiles, axis=1)
    cut = lambda value: [value[:, t * LANES : (t + 1) * LANES] for t in range(tiles_x)]

    for h in range(offsets):
        image[h] = jnp.zeros((cells_z, cells_x), jnp.float32) if start else before[h]

    def one(j, carry):
        shot, z = j // (cells_z // rows), lax.rem(j, cells_z // rows)
        at = pl.ds(pl.multiple_of(z * rows, rows), rows)
        for m in range(snaps):
            receiver = cut(held[shot, m * fields + 1, at])
            for b in range(offsets // FINE):
                coarse[m, b] = join(turned_x(receiver, FINE * b - half, lane))
            source = cut(held[shot, m * fields, at])
            for a in range(FINE):
                fine[m, a] = join(turned_x(source, -a, lane))
        for a in range(FINE):
            for b in range(offsets // FINE):
                total = image[FINE * b + a, at]
                for m in range(snaps):
                    total += fine[m, a] * coarse[m, b]
                image[FINE * b + a, at] = total
        return carry

    lax.fori_loop(0, place * (cells_z // rows), one, 0)
    if not finish:
        return
    lane = lax.broadcasted_iota(jnp.int32, (cells_z, LANES), 1)
    for k, out in enumerate(outs):
        tail = (snaps if k < NEAR else 1) * fields * cells_z
        ends = arrays[k][pl.ds(tail, TAIL)].astype(jnp.float32)
        for i in range(out.shape[0]):
            lag = ends[i, 0].astype(jnp.int32)
            place = half + lag
            back = lax.rem(place, FINE)
            tiles = [image[place, :, pl.ds(t * LANES, LANES)] for t in range(tiles_x)]
            rolled = [pltpu.roll(tile, lax.rem(LANES - back, LANES), 1) for tile in tiles]
            keep = lane < LANES - back
            for t in range(tiles_x):
                x = lane + (t * LANES + lag)
                value = jnp.where(keep, rolled[t], rolled[(t + 1) % tiles_x])
                value = jnp.where((x >= 0) & (x < cells_x), value, 0.0)
                out[i, :, pl.ds(t * LANES, LANES)] = value.astype(out.dtype)


def wanted(ours, groups, snaps, finish):
    names = {name for k in ours for name, _ in found_at(k, snaps, 1, 1)}
    return sorted(names | (set(range(groups)) if finish else set()))


def imaged(spec, valid, parts, before, offsets):
    ours, groups, snaps, fields, start, finish = spec
    rows, cells_x = parts[0].shape
    cells_z = (rows - TAIL) // (snaps * fields)
    shape = jax.ShapeDtypeStruct
    if finish:
        per_group = offsets // groups
        outs = [shape((per_group, cells_z, cells_x), jnp.bfloat16)] * groups
        outs[0] = shape((per_group, cells_z, cells_x), jnp.float32)
    else:
        outs = [shape((offsets, cells_z, cells_x), jnp.float32)]
    args = [valid, *[parts[name] for name in wanted(ours, groups, snaps, finish)]]
    args += [] if start else [before]
    scratch = [pltpu.VMEM((offsets, cells_z, cells_x), jnp.float32)] if finish else []
    strip = (2 * SUBLANES, cells_x)
    made = pl.pallas_call(
        functools.partial(image_kernel, spec),
        out_shape=outs,
        in_specs=[SMEM] + [VMEM] * (len(args) - 1),
        out_specs=[VMEM] * len(outs),
        scratch_shapes=[
            *scratch,
            pltpu.VMEM((len(ours), snaps * fields, cells_z, cells_x), jnp.float32),
            pltpu.VMEM((snaps, offsets // FINE, *strip), jnp.float32),
            pltpu.VMEM((snaps, FINE, *strip), jnp.float32),
        ],
        compiler_params=pltpu.CompilerParams(vmem_limit_bytes=8 * 1024 * 1024),
        cost_estimate=pl.CostEstimate(
            flops=200 * snaps * len(ours) * offsets * cells_z * cells_x,
            bytes_accessed=8 * offsets * cells_z * cells_x,
            transcendentals=0,
        ),
        name="image",
    )(*args)
    return made if finish else made[0]


def gather_kernel(me_ref, *refs):
    out_ref = refs[-1]
    for k, part_ref in enumerate(refs[:-1]):
        y = jnp.bitwise_xor(me_ref[0], k)
        for i in range(out_ref.shape[0]):
            out_ref[i, y] = part_ref[i].astype(jnp.float32)


def far_first(groups, giving=False):
    order = (6, 7, 1, 2, 5, 4, 3) if giving else (6, 7, 5, 4, 2, 3, 1)
    return [k for k in order if k < groups] + [k for k in range(8, groups)]


def on_device_planes(checkpoint, traces, courant_sq, holder, offset_lags):
    start = checkpoint[0]
    fields, planes, cells_z, cells_x = start.shape[1:]
    step_count = traces.shape[1]
    groups = lax.axis_size("off")
    per_group = offset_lags.shape[1]
    snaps = step_count // 2
    me = lax.axis_index("off").astype(jnp.int32)
    side = lax.axis_index("gy").astype(jnp.int32)
    slots = jnp.bitwise_xor(me, jnp.arange(groups, dtype=jnp.int32))
    valid = jnp.any(holder[None, :] == slots[:, None], axis=1).astype(jnp.int32)
    side1, me1 = side.reshape(1), me.reshape(1)
    swap = [(0, 1), (1, 0)]

    apart = jnp.abs(
        lax.broadcasted_iota(jnp.int32, (cells_x, cells_x), 0)
        - lax.broadcasted_iota(jnp.int32, (cells_x, cells_x), 1)
    )
    band = jnp.zeros((cells_x, cells_x), jnp.float32)
    for tap in range(1, REACH + 1):
        band = jnp.where(apart == tap, TAPS[tap], band)
    band = band.astype(jnp.bfloat16)

    edge = lax.dynamic_slice(
        checkpoint,
        (0, 1, 0, (1 - side) * (planes - REACH), 0, 0),
        (1, 1, fields, REACH, cells_z, cells_x),
    )[0, 0]
    earlier = current = None
    drive = jnp.where(side >= 0, traces[0], 0.0)
    constant = [courant_sq * (BAND_UNIT / COMMON), drive, band]
    early = {}

    def pairs(k):
        return [(i, i ^ k) for i in range(groups)]

    for n in range(step_count):
        halo = lax.ppermute(edge, "gy", swap)
        last = n == step_count - 1
        levels = [start] if n == 0 else [start, current] if n == 1 else [earlier, current]
        fresh = half_step((n, False, last), side1, [], constant, levels, [], groups)[0]
        extra = [me1, offset_lags] if last or n == 1 else []
        made = half_step(
            (n, True, last), side1, extra, constant, levels, [halo, fresh], groups
        )
        if not last:
            earlier, current, edge = current, made[0], made[1]
        if n == 1:
            for i, k in enumerate(FAR):
                early[-1 - i] = lax.ppermute(made[2 + i], "off", pairs(k))
    parts = list(made)
    parts[1] = relayed(parts[1], [early[-1 - i] for i in range(len(FAR))])

    order = far_first(groups, True)
    got, back = {0: parts[0], **early}, {}
    for k in order:
        got[k] = lax.ppermute(parts[k], "off", pairs(k))
    offsets = groups * per_group
    stages = ((0, 6, 1, 2, 7, 5), (4, 3))
    images = None
    for i, ours in enumerate(stages):
        spec = (ours, groups, snaps, fields, i == 0, i == len(stages) - 1)
        images = imaged(spec, valid, got, images, offsets)
    for k in far_first(groups):
        back[k] = lax.ppermute(images[k], "off", pairs(k))
    back[0] = images[0]
    return pl.pallas_call(
        gather_kernel,
        out_shape=jax.ShapeDtypeStruct((per_group, planes, cells_z, cells_x), jnp.float32),
        in_specs=[SMEM] + [VMEM] * groups,
        out_specs=VMEM,
        compiler_params=pltpu.CompilerParams(vmem_limit_bytes=8 * 1024 * 1024),
        name="gather",
    )(me1, *[back[k] for k in range(groups)])


def solution(mesh):
    placed = (
        P(("survey", "off"), None, None, "gy", None, None),
        P(("survey", "off"), None, "gy", None),
        P("gy", None, None),
        P("survey"),
        P(("survey", "off"), None),
    )

    def on_device(checkpoint, traces, courant_sq, holder, offset_lags):
        groups, sides = mesh.shape["off"], mesh.shape["gy"]
        planes, cells_z, cells_x = courant_sq.shape
        fits = (
            groups == planes
            and groups == NEAR + 2 * len(FAR)
            and sides == 2
            and planes == 2 * REACH
            and cells_z % (2 * SUBLANES) == 0
            and cells_x % LANES == 0
            and cells_x >= 2 * LANES
            and traces.shape[1] == 4
            and groups * offset_lags.shape[1] <= LANES
            and offset_lags.shape[1] <= SUBLANES
        )
        chosen = on_device_planes if fits else on_device_general
        return chosen(checkpoint, traces, courant_sq, holder, offset_lags)

    return jax.shard_map(
        on_device,
        mesh=mesh,
        in_specs=placed,
        out_specs=P(("survey", "off"), "gy", None, None),
        check_vma=False,
    )
```
